256 devices in a mesh: leaf: 128 (over y, x, z), rhs: 2 (over core).
Axes of the slice: x: 4, y: 4, z: 8, core: 2. Of those that a mesh axis runs over, the one named last changes fastest.
Arguments:
- rhs_block: bfloat16 [2048, 128, 256], P('leaf', 'rhs'), may hold values from -6 to 6
- basis: bfloat16 [2048, 256, 256], P(('leaf', 'rhs')), may hold values from -0.375 to 0.375
- red_inverse: bfloat16 [2048, 192, 192], P(('leaf', 'rhs')), may hold values from -0.4375 to 0.4375
- forward_coupling: bfloat16 [2048, 64, 1536], P(('leaf', 'rhs')), may hold values from -0.15625 to 0.15625
- backward_coupling: bfloat16 [2048, 192, 512], P(('leaf', 'rhs')), may hold values from -0.25 to 0.25
- parent_inverse: bfloat16 [1024, 128, 128], P(('leaf', 'rhs')), may hold values from -0.5 to 0.5
- near_index: int32 [2048, 8], P('leaf'), may hold values from 0 to 2047, as said below
- near_count: int32 [2048], P('leaf'), may hold values from 1 to 8, as said below
Outputs:
- solution: bfloat16 [2048, 128, 256], P('leaf', 'rhs')
The draws below stay inside these ranges and needn't reach their ends.
Inputs may be any that keep to these rules, and one draw needn't show every extreme that they name: `near_index`: every slot, used or not, names a cluster other than its own whose distance from it in tree order is at most 32; some slot in every draw is at distance 32. Slots k >= near_count[c] of cluster c are unused.
All inputs are finite; a program needn't handle non-finite values.
Results may differ from the reference program's by a relative error of at most 0.007.
Values may be sent and summed in bfloat16 or wider, within the bound.
No kernel may reach another device: no remote copies, remote signals or barrier semaphores. Data moves between devices by JAX's collectives and lax.ppermute only.
A program may use at most 64 MiB of HBM per device.

```python
import math
import jax
import jax.numpy as jnp
from jax import lax

L = 256
K = 64
R = 192
NRHS = 128
NEAR = 8
CL_DEV = 16
CLUSTERS = 2048
PARENTS = 1024
SPAN = 32


def near_lists(key):
    folded = jax.random.fold_in(key, 11)
    subkeys = jax.random.split(folded, 4)
    cluster_total = CLUSTERS
    magnitude = jax.random.randint(subkeys[0], (cluster_total, NEAR), 1, SPAN + 1)
    direction = jax.random.randint(subkeys[1], (cluster_total, NEAR), 0, 2) * 2 - 1
    offsets = magnitude * direction
    anchor = jnp.arange(cluster_total, dtype=jnp.int32)[:, None]
    target = anchor + offsets
    target = jnp.where((target < 0) | (target >= cluster_total), anchor - offsets, target)
    target = target.at[0, 0].set(SPAN)
    crowded = jax.random.randint(subkeys[2], (cluster_total // CL_DEV,), 0, 4) == 0
    crowded = jnp.repeat(crowded, CL_DEV)
    counts = jax.random.randint(subkeys[3], (cluster_total,), 1, 5)
    counts = jnp.where(crowded, NEAR, counts)
    counts = counts.at[0].set(NEAR)
    return (target.astype(jnp.int32), counts.astype(jnp.int32))


def draw_near_index(key, part):
    return near_lists(key)[0]


def draw_near_count(key, part):
    return near_lists(key)[1]


def shard_levels(key, dims, cuts, low, largest):
    factor_of = 1.0
    for position, blocks in cuts:
        heights = jax.random.uniform(jax.random.fold_in(jax.random.fold_in(key, 6), position), (blocks,), jnp.float32, low / len(cuts), largest / len(cuts))
        factor_of = factor_of * jnp.repeat(jnp.exp(heights), dims[position] // blocks).reshape((-1,) + (1,) * (len(dims) - 1 - position))
    return factor_of


def bell_draw(stream_key, extent, spread, bound, cuts=(), held_as=jnp.bfloat16):
    values = spread * jax.random.normal(stream_key, extent, jnp.float32)
    if cuts:
        values = values * shard_levels(stream_key, extent, cuts, -0.22, 0.18)
    return jnp.clip(values, -bound, bound).astype(held_as)


def setup_inputs(seed: int = 0) -> dict:
    splits = jax.random.split(jax.random.key(seed), 9)
    return {
        "rhs_block": bell_draw(splits[0], (CLUSTERS, NRHS, L), 1.0, 6.0, ((0, 128), (1, 2))),
        "basis": bell_draw(splits[1], (CLUSTERS, L, L), L ** -0.5, 0.375, ((0, 256),)),
        "red_inverse": bell_draw(splits[2], (CLUSTERS, R, R), R ** -0.5, 0.4375, ((0, 256),)),
        "forward_coupling": bell_draw(splits[3], (CLUSTERS, K, NEAR * R), (NEAR * R) ** -0.5, 0.15625, ((0, 256),)),
        "backward_coupling": bell_draw(splits[4], (CLUSTERS, R, NEAR * K), (NEAR * K) ** -0.5, 0.25, ((0, 256),)),
        "parent_inverse": bell_draw(splits[5], (PARENTS, 2 * K, 2 * K), (2 * K) ** -0.5, 0.5, ((0, 256),)),
        "near_index": draw_near_index(jax.random.fold_in(splits[8], 71), 0),
        "near_count": draw_near_count(jax.random.fold_in(splits[8], 71), 0),
    }


def rounded(values):
    return lax.optimization_barrier(values.astype(jnp.bfloat16))


def reference(rhs_block, basis, red_inverse, forward_coupling, backward_coupling, parent_inverse, near_index, near_count):
    single = jnp.float32
    width_block = math.gcd(CLUSTERS, 64)
    groups = CLUSTERS // width_block

    def grouped(array):
        return array.reshape((groups, width_block) + array.shape[1:])

    def forward_local(pieces):
        right_side, basis_part, inverse_part = pieces
        projected = jnp.einsum("cna,cab->cnb", right_side.astype(single), basis_part.astype(single))
        redundant = rounded(projected[..., :R])
        eliminated = rounded(jnp.einsum("cnr,cqr->cnq", redundant.astype(single), inverse_part.astype(single)))
        return eliminated, projected[..., R:]

    eliminated, skeleton_rows = lax.map(forward_local, (grouped(rhs_block), grouped(basis), grouped(red_inverse)))
    eliminated = eliminated.reshape(CLUSTERS, NRHS, R)
    skeleton_rows = skeleton_rows.reshape(CLUSTERS, NRHS, K)
    in_use = jnp.arange(NEAR, dtype=jnp.int32)[None, :] < near_count[:, None]

    def couple(pieces):
        indices, used_part, coupling_part, skeleton_part = pieces
        picked = jnp.take(eliminated, indices.reshape(-1), axis=0).reshape(width_block, NEAR, NRHS, R)
        picked = jnp.where(used_part[:, :, None, None], picked.astype(single), 0.0)
        blocks = coupling_part.astype(single).reshape(width_block, K, NEAR, R)
        return rounded(skeleton_part - jnp.einsum("ckna,cqka->cnq", picked, blocks))

    reduced = lax.map(couple, (grouped(near_index), grouped(in_use), grouped(forward_coupling), grouped(skeleton_rows)))
    reduced = reduced.reshape(CLUSTERS, NRHS, K)
    paired = jnp.concatenate([reduced[0::2], reduced[1::2]], axis=-1)
    solved = rounded(jnp.einsum("pnq,pmq->pnm", paired.astype(single), parent_inverse.astype(single)))
    skeleton_solution = jnp.stack([solved[..., :K], solved[..., K:]], axis=1).reshape(CLUSTERS, NRHS, K)

    def backward_local(pieces):
        indices, used_part, coupling_part, eliminated_part, inverse_part, basis_part, own_skeleton = pieces
        picked = jnp.take(skeleton_solution, indices.reshape(-1), axis=0).reshape(width_block, NEAR, NRHS, K)
        picked = jnp.where(used_part[:, :, None, None], picked.astype(single), 0.0)
        blocks = coupling_part.astype(single).reshape(width_block, R, NEAR, K)
        corrected = rounded(eliminated_part.astype(single) - jnp.einsum("ckna,crka->cnr", picked, blocks))
        recovered = rounded(jnp.einsum("cnq,cqr->cnr", corrected.astype(single), inverse_part.astype(single)))
        combined = jnp.concatenate([recovered, own_skeleton], axis=-1).astype(single)
        return jnp.einsum("cnb,cab->cna", combined, basis_part.astype(single)).astype(jnp.bfloat16)

    solution = lax.map(backward_local, (grouped(near_index), grouped(in_use), grouped(backward_coupling), grouped(eliminated), grouped(red_inverse), grouped(basis), grouped(skeleton_solution)))
    return solution.reshape(CLUSTERS, NRHS, L)
```

```python
import jax
import jax.numpy as jnp
from jax import lax
from jax.experimental import pallas as pl
from jax.experimental.pallas import tpu as pltpu
from jax.sharding import PartitionSpec as P

HALF = 64
F32 = jnp.float32
BF16 = jnp.bfloat16
NT = (((1,), (1,)), ((), ()))


def both_ways(pairs):
    return [(a, b) for a, b in pairs] + [(b, a) for a, b in pairs]


def leaf_pairs(count):
    inner = both_ways([(i, i + 1) for i in range(0, count - 1, 2)])
    outer = both_ways([(i, i + 1) for i in range(1, count - 1, 2)])
    near = both_ways([(i, i + 2) for i in range(count - 2) if i % 4 in (0, 1)])
    far = both_ways([(i, i + 2) for i in range(count - 2) if i % 4 in (2, 3)])
    return inner, outer, near, far


def swap(value):
    return lax.ppermute(value, "rhs", [(0, 1), (1, 0)])


def along(value, pairs):
    return lax.ppermute(value, "leaf", pairs)


def lanes(shape):
    return lax.broadcasted_iota(jnp.int32, shape, len(shape) - 1)


def spot(near_ref, count_ref, cluster, k, leaf, core):
    target = near_ref[k, cluster]
    away = (lax.shift_right_logical(target, 4) - leaf) * (1 - 2 * (leaf & 1))
    block = jnp.where(away > 0, 2 * away - 1, -2 * away)
    inside = target & 15
    chunk = lax.shift_right_logical(inside, 3) ^ core
    used = k < count_ref[cluster]
    return block, chunk, inside & 7, used


def lane_mask(which, used):
    lane = lanes((1, 2 * HALF))
    first = which * HALF
    return jnp.where((lane >= first) & (lane < first + HALF) & used, 1.0, 0.0).astype(BF16)


def project_kernel(other, rhs_ref, basis_ref, inverse_ref, elim_ref, skel_ref):
    core = lax.axis_index("rhs")
    base = ((1 - core) if other else core) * 8
    redundant = inverse_ref.shape[1]
    zeros = jnp.zeros((HALF, redundant), BF16)
    for pair in range(4):
        elim = None
        tails = []
        for t in range(2):
            j = 2 * pair + t
            projected = jnp.dot(rhs_ref[base + j], basis_ref[j], preferred_element_type=F32)
            head = projected[:, :redundant].astype(BF16)
            tails.append(projected[:, 128:])
            stack = [head, zeros] if t == 0 else [zeros, head]
            part = lax.dot_general(
                inverse_ref[j], jnp.concatenate(stack, axis=0), NT, preferred_element_type=F32
            )
            elim = part if elim is None else elim + part
        elim_ref[pair] = elim.astype(BF16)
        skel_ref[pair] = jnp.concatenate(tails, axis=0).T[HALF:, :]


def project(rhs_block, basis, inverse, other):
    import functools

    return pl.pallas_call(
        functools.partial(project_kernel, other),
        out_shape=(
            jax.ShapeDtypeStruct((4, 192, 128), BF16),
            jax.ShapeDtypeStruct((4, 64, 128), F32),
        ),
        name="project",
        cost_estimate=pl.CostEstimate(flops=2 * 8 * 64 * (65536 + 36864), bytes_accessed=2500000, transcendentals=0),
        compiler_params=pltpu.CompilerParams(vmem_limit_bytes=6 << 20),
    )(rhs_block, basis, inverse)


def reduce_kernel(near_ref, count_ref, *refs):
    blocks = refs[:10]
    f_refs = refs[10:12]
    skel_refs = refs[12:14]
    parent_refs = refs[14:16]
    out_ref = refs[16]
    window, sems = refs[17:]
    copies = []
    for n, block in enumerate(blocks):
        copies.append(pltpu.make_async_copy(block, window.at[pl.ds(4 * n, 4)], sems.at[n]))
    for copy in copies:
        copy.start()
    for copy in copies:
        copy.wait()
    leaf, core = lax.axis_index("leaf"), lax.axis_index("rhs")
    low = lanes((1, 2 * HALF)) < HALF
    for h in range(2):
        base = (core ^ h) * 8
        for two in range(2):
            solved = []
            for parity in range(2):
                pair = 2 * two + parity
                skel = skel_refs[h][pair]
                turned = pltpu.roll(skel, HALF, 1)
                reduced = []
                for t in range(2):
                    j = 2 * pair + t
                    parts = []
                    for k in range(8):
                        block, chunk, inside, used = spot(near_ref, count_ref, base + j, k, leaf, core)
                        row = block * 8 + chunk * 4 + lax.shift_right_logical(inside, 1)
                        parts.append(window[row] * lane_mask(inside & 1, used))
                    total = jnp.dot(f_refs[h][j], jnp.concatenate(parts, axis=0), preferred_element_type=F32)
                    total = total + pltpu.roll(total, HALF, 1)
                    reduced.append(((skel if t == parity else turned) - total).astype(BF16))
                solved.append(
                    jnp.dot(
                        parent_refs[h][pair], jnp.concatenate(reduced, axis=0), preferred_element_type=F32
                    )
                )
            out_ref[2 * h + two] = jnp.where(low, solved[0], solved[1]).astype(BF16)


def reduce_and_solve(near_index, near_count, blocks, forward, skel, parent):
    smem = pl.BlockSpec(memory_space=pltpu.SMEM)
    vmem = pl.BlockSpec(memory_space=pltpu.VMEM)
    anywhere = pl.BlockSpec(memory_space=pl.ANY)
    return pl.pallas_call(
        reduce_kernel,
        out_shape=jax.ShapeDtypeStruct((4, 128, 128), BF16),
        in_specs=[smem, smem] + [anywhere] * 10 + [vmem] * 6,
        scratch_shapes=[pltpu.VMEM((40, 192, 128), BF16), pltpu.SemaphoreType.DMA((10,))],
        name="reduce_and_solve",
        cost_estimate=pl.CostEstimate(flops=2 * 16 * 64 * 1536 * 128, bytes_accessed=6000000, transcendentals=0),
        compiler_params=pltpu.CompilerParams(vmem_limit_bytes=8 << 20),
    )(near_index, near_count, *blocks, *forward, *skel, *parent)


def finish_kernel(near_ref, count_ref, *refs):
    blocks = refs[:5]
    b_refs = refs[5:7]
    elim_refs = refs[7:9]
    inverse_refs = refs[9:11]
    basis_refs = refs[11:13]
    out_ref = refs[13]
    window, sems = refs[14:]
    copies = []
    for n, block in enumerate(blocks):
        copies.append(pltpu.make_async_copy(block, window.at[pl.ds(4 * n, 4)], sems.at[n]))
    for copy in copies:
        copy.start()
    for copy in copies:
        copy.wait()
    leaf, core = lax.axis_index("leaf"), lax.axis_index("rhs")
    flip = jnp.where((leaf & 3 == 1) | (leaf & 3 == 2), 7, 0)
    low = lanes((1, 2 * HALF)) < HALF
    for h in range(2):
        base = (core ^ h) * 8
        for two in range(2):
            own = window[2 * h + two].T
            for parity in range(2):
                pair = 2 * two + parity
                own_part = own[parity * HALF : (parity + 1) * HALF, :]
                carried = []
                for t in range(2):
                    j = 2 * pair + t
                    parts = []
                    for k in range(8):
                        block, chunk, inside, used = spot(near_ref, count_ref, base + j, k, leaf, core)
                        block = jnp.where(block >= 3, block ^ flip, block)
                        row = block * 4 + chunk * 2 + lax.shift_right_logical(inside, 2)
                        place = pl.multiple_of((inside & 1) * HALF, HALF)
                        which = lax.shift_right_logical(inside, 1) & 1
                        parts.append(window[row, pl.ds(place, HALF), :] * lane_mask(which, used))
                    total = jnp.dot(b_refs[h][j], jnp.concatenate(parts, axis=0), preferred_element_type=F32)
                    carried.append(total + pltpu.roll(total, HALF, 1))
                corrected = elim_refs[h][pair].astype(F32) - jnp.where(low, carried[0], carried[1])
                corrected = corrected.T.astype(BF16)
                for t in range(2):
                    j = 2 * pair + t
                    rows = corrected[t * HALF : (t + 1) * HALF, :]
                    recovered = jnp.dot(rows, inverse_refs[h][j], preferred_element_type=F32).astype(BF16)
                    combined = jnp.concatenate([recovered, own_part[:, t * HALF : (t + 1) * HALF]], axis=1)
                    out_ref[base + j] = lax.dot_general(
                        combined, basis_refs[h][j], NT, preferred_element_type=F32
                    ).astype(BF16)


def finish(near_index, near_count, blocks, backward, elim, inverse, basis):
    smem = pl.BlockSpec(memory_space=pltpu.SMEM)
    vmem = pl.BlockSpec(memory_space=pltpu.VMEM)
    anywhere = pl.BlockSpec(memory_space=pl.ANY)
    return pl.pallas_call(
        finish_kernel,
        out_shape=jax.ShapeDtypeStruct((16, 64, 256), BF16),
        in_specs=[smem, smem] + [anywhere] * 5 + [vmem] * 8,
        scratch_shapes=[pltpu.VMEM((20, 128, 128), BF16), pltpu.SemaphoreType.DMA((5,))],
        name="finish",
        cost_estimate=pl.CostEstimate(flops=2 * 16 * 192 * 512 * 128, bytes_accessed=8000000, transcendentals=0),
        compiler_params=pltpu.CompilerParams(vmem_limit_bytes=8 << 20),
    )(near_index, near_count, *blocks, *backward, *elim, *inverse, *basis)


def on_device(
    rhs_block,
    basis,
    red_inverse,
    forward_coupling,
    backward_coupling,
    parent_inverse,
    near_index,
    near_count,
):
    inner, outer, near, far = leaf_pairs(lax.axis_size("leaf"))
    basis_b, inverse_b = swap(basis), swap(red_inverse)
    elim_a, skel_a = project(rhs_block, basis, red_inverse, False)
    outer_a = along(elim_a, outer)
    inner_a = along(elim_a, inner)
    elim_b, skel_b = project(rhs_block, basis_b, inverse_b, True)
    outer_b = along(elim_b, outer)
    inner_b = along(elim_b, inner)
    forward_b, parent_b, backward_b = swap(forward_coupling), swap(parent_inverse), swap(backward_coupling)
    far_outer_a = along(inner_a, outer)
    far_inner_a = along(outer_a, inner)
    far_outer_b = along(inner_b, outer)
    far_inner_b = along(outer_b, inner)
    blocks = (
        elim_a, elim_b, inner_a, inner_b, outer_a, outer_b,
        far_inner_a, far_inner_b, far_outer_a, far_outer_b,
    )
    skeleton = reduce_and_solve(
        near_index.T, near_count, blocks, (forward_coupling, forward_b), (skel_a, skel_b), (parent_inverse, parent_b)
    )
    outer_s = along(skeleton, outer)
    far_s = along(skeleton, far)
    inner_s = along(skeleton, inner)
    near_s = along(skeleton, near)
    return finish(
        near_index.T, near_count, (skeleton, inner_s, outer_s, near_s, far_s),
        (backward_coupling, backward_b), (elim_a, elim_b), (red_inverse, inverse_b), (basis, basis_b),
    )


def solution(mesh):
    whole = P(("leaf", "rhs"), None, None)
    in_specs = (P("leaf", "rhs", None), whole, whole, whole, whole, whole, P("leaf", None), P("leaf"))
    return jax.shard_map(
        on_device, mesh=mesh, in_specs=in_specs, out_specs=P("leaf", "rhs", None), check_vma=False
    )
```

```python
import functools

import jax
import jax.numpy as jnp
from jax import lax
from jax.experimental import pallas as pl
from jax.experimental.pallas import tpu as pltpu
from jax.sharding import PartitionSpec as P


HALF = 64
ROWS = 40
F32 = jnp.float32
BF16 = jnp.bfloat16
NT = (((1,), (1,)), ((), ()))
SMEM = pl.BlockSpec(memory_space=pltpu.SMEM)
VMEM = pl.BlockSpec(memory_space=pltpu.VMEM)
HBM = pl.BlockSpec(memory_space=pltpu.HBM)


def shape(*dims, dtype=BF16):
    return jax.ShapeDtypeStruct(dims, dtype)


def cost(flops, moved):
    return pl.CostEstimate(flops=flops, bytes_accessed=moved, transcendentals=0)


def limit(mebibytes):
    return pltpu.CompilerParams(vmem_limit_bytes=mebibytes << 20)


def in_hbm(*values):
    return [pltpu.with_memory_space_constraint(value, pltpu.HBM) for value in values]


def both_ways(pairs):
    return [(a, b) for a, b in pairs] + [(b, a) for a, b in pairs]


def leaf_pairs(count):
    inner = both_ways([(i, i + 1) for i in range(0, count - 1, 2)])
    outer = both_ways([(i, i + 1) for i in range(1, count - 1, 2)])
    near = both_ways([(i, i + 2) for i in range(count - 2) if i % 4 in (0, 1)])
    far = both_ways([(i, i + 2) for i in range(count - 2) if i % 4 in (2, 3)])
    return inner, outer, near, far


def swap(value):
    return lax.ppermute(value, "rhs", [(0, 1), (1, 0)])


def along(value, pairs):
    return lax.ppermute(value, "leaf", pairs)


def low_lanes():
    return lax.broadcasted_iota(jnp.int32, (1, 2 * HALF), 1) < HALF


def turned(value):
    return pltpu.roll(value, HALF, 1)


def tables_kernel(near_ref, count_ref, forward_ref, backward_ref):
    leaf, core = lax.axis_index("leaf"), lax.axis_index("rhs")
    sign = 1 - 2 * (leaf & 1)
    flip = jnp.where((leaf & 3 == 1) | (leaf & 3 == 2), 7, 0)
    target = near_ref[...]
    slot = lax.broadcasted_iota(jnp.int32, target.shape, 0)
    cluster = lax.broadcasted_iota(jnp.int32, target.shape, 1)
    used = slot < count_ref[...]
    away = (lax.shift_right_logical(target, 4) - leaf) * sign
    block = jnp.where(away > 0, 2 * away - 1, -2 * away)
    other = jnp.where(block >= 3, block ^ flip, block)
    inside = target & 15
    place = lax.shift_right_logical(inside ^ (core << 3), 1)
    side = inside & 1
    forward = block * 8 + place + (side ^ (lax.shift_right_logical(cluster, 1) & 1)) * ROWS
    backward = other * 8 + place + (side ^ (slot & 1)) * ROWS
    forward_ref[...] = jnp.where(used, forward, 2 * ROWS)
    backward_ref[...] = jnp.where(used, backward, 2 * ROWS)


def tables(near_index, near_count):
    slots = near_index.T
    return pl.pallas_call(
        tables_kernel,
        out_shape=[shape(*slots.shape, dtype=jnp.int32)] * 2,
        in_specs=[VMEM] * 2,
        out_specs=[VMEM] * 2,
        name="tables",
        cost_estimate=cost(10000, 10000),
        compiler_params=limit(1),
    )(slots, near_count.reshape(1, -1))


def project_pair(pair, base, rhs_ref, basis_ref, inverse_ref, elim_ref, skel_ref):
    redundant = inverse_ref.shape[1]
    zeros = jnp.zeros((HALF, redundant), BF16)
    elim = None
    tails = []
    for t in range(2):
        j = 2 * pair + t
        projected = jnp.dot(rhs_ref[base + j], basis_ref[j], preferred_element_type=F32)
        head = projected[:, :redundant].astype(BF16)
        tails.append(projected[:, 128:])
        stack = [head, zeros] if t == 0 else [zeros, head]
        part = lax.dot_general(
            inverse_ref[j], jnp.concatenate(stack, axis=0), NT, preferred_element_type=F32
        )
        elim = part if elim is None else elim + part
    elim_ref[pair] = elim.astype(BF16)
    skel_ref[pair] = jnp.concatenate(tails, axis=0).T[HALF:, :]


def project_own_kernel(
    rhs_hbm, basis_hbm, inverse_hbm, elim_ref, skel_ref, rest_ref, basis, inverse, rhs, sems, rest_sem
):
    core = lax.axis_index("rhs")
    base = core * 8
    copies = []
    for pair in range(4):
        here = pl.ds(2 * pair, 2)
        group = [
            pltpu.make_async_copy(rhs_hbm.at[pl.ds(base + 2 * pair, 2)], rhs.at[here], sems.at[pair, 0]),
            pltpu.make_async_copy(basis_hbm.at[here], basis.at[here], sems.at[pair, 1]),
            pltpu.make_async_copy(inverse_hbm.at[here], inverse.at[here], sems.at[pair, 2]),
        ]
        for copy in group:
            copy.start()
        copies.append(group)
    rest = pltpu.make_async_copy(rhs_hbm.at[pl.ds(8 - base, 8)], rest_ref, rest_sem)
    rest.start()
    for group in copies:
        for copy in group:
            copy.wait()
    for pair in range(4):
        project_pair(pair, 0, rhs, basis, inverse, elim_ref, skel_ref)
    rest.wait()


def project_own(rhs_block, basis, inverse):
    return pl.pallas_call(
        project_own_kernel,
        out_shape=[
            shape(4, 192, 128),
            shape(4, 64, 128, dtype=F32),
            shape(8, *rhs_block.shape[1:]),
            shape(*basis.shape),
            shape(*inverse.shape),
        ],
        in_specs=[HBM] * 3,
        out_specs=[VMEM] * 5,
        scratch_shapes=[
            pltpu.VMEM((8,) + rhs_block.shape[1:], BF16),
            pltpu.SemaphoreType.DMA((4, 3)),
            pltpu.SemaphoreType.DMA(()),
        ],
        name="project_own",
        cost_estimate=cost(2 * 8 * 64 * (65536 + 36864), 2500000),
        compiler_params=limit(8),
    )(*in_hbm(rhs_block, basis, inverse))


def project_other_kernel(rhs_ref, basis_ref, inverse_ref, elim_ref, skel_ref):
    for pair in range(4):
        project_pair(pair, 0, rhs_ref, basis_ref, inverse_ref, elim_ref, skel_ref)


def project_other(rhs_block, basis, inverse):
    return pl.pallas_call(
        project_other_kernel,
        out_shape=[shape(4, 192, 128), shape(4, 64, 128, dtype=F32)],
        in_specs=[VMEM] * 3,
        out_specs=[VMEM] * 2,
        name="project_other",
        cost_estimate=cost(2 * 8 * 64 * (65536 + 36864), 2500000),
        compiler_params=limit(6),
    )(rhs_block, basis, inverse)


def place_block(window, block, first):
    for pair in range(block.shape[0]):
        value = block[pair]
        window[first + pair] = value
        window[first + pair + ROWS] = turned(value)


def gather_kernel(firsts, fresh, *refs):
    window = refs[-1]
    blocks = refs[:-1] if fresh else refs[1:-1]
    for first, block in zip(firsts, blocks):
        place_block(window, block, first)
    if fresh:
        window[2 * ROWS] = jnp.zeros(window.shape[1:], BF16)


def gather(firsts, blocks, window=None):
    fresh = window is None
    operands = blocks if fresh else (window,) + blocks
    return pl.pallas_call(
        functools.partial(gather_kernel, firsts, fresh),
        out_shape=shape(2 * ROWS + 1, 192, 128),
        in_specs=[VMEM] * len(operands),
        out_specs=VMEM,
        input_output_aliases={} if fresh else {0: 0},
        name="gather",
        cost_estimate=cost(1000, 4000000),
        compiler_params=limit(6),
    )(*operands)


def fold_kernel(elim_ref, inverse_ref, basis_ref, backward_ref, wide_ref, base_ref, tail_ref):
    redundant = inverse_ref.shape[1]
    for pair in range(4):
        elim = elim_ref[pair].astype(F32).T.astype(BF16)
        for t in range(2):
            j = 2 * pair + t
            both = lax.dot_general(
                basis_ref[j][:, :redundant], inverse_ref[j], NT, preferred_element_type=F32
            ).astype(BF16)
            wide_ref[j] = jnp.dot(both, backward_ref[j], preferred_element_type=F32).astype(BF16)
            base_ref[j] = lax.dot_general(
                elim[t * HALF : (t + 1) * HALF, :], both, NT, preferred_element_type=F32
            )
            tail_ref[j] = basis_ref[j][:, 128:]


def fold(elim, inverse, basis, backward):
    return pl.pallas_call(
        fold_kernel,
        out_shape=(shape(8, 256, 512), shape(8, 64, 256, dtype=F32), shape(8, 256, 128)),
        in_specs=[VMEM] * 4,
        out_specs=[VMEM] * 3,
        name="fold",
        cost_estimate=cost(2 * 8 * 256 * 192 * 768, 8000000),
        compiler_params=limit(6),
    )(elim, inverse, basis, backward)


def reduce_kernel(table_ref, window_in, *refs):
    blocks = refs[:2]
    f_refs = refs[2:4]
    skel_refs = refs[4:6]
    parent_refs = refs[6:8]
    out_ref, window = refs[8:]
    core = lax.axis_index("rhs")
    for first, block in zip((28, 36), blocks):
        place_block(window, block, first)
    low = low_lanes()
    for h in range(2):
        for two in range(2):
            solved = []
            for parity in range(2):
                pair = 2 * two + parity
                skel = skel_refs[h][pair]
                reduced = []
                for t in range(2):
                    j = 2 * pair + t
                    parts = [window[table_ref[k, (core ^ h) * 8 + j]] for k in range(8)]
                    total = jnp.dot(
                        f_refs[h][j], jnp.concatenate(parts, axis=0), preferred_element_type=F32
                    )
                    reduced.append(((skel if t == parity else turned(skel)) - total).astype(BF16))
                solved.append(
                    jnp.dot(
                        parent_refs[h][pair], jnp.concatenate(reduced, axis=0), preferred_element_type=F32
                    )
                )
            both = jnp.where(low, solved[0], solved[1]).T.astype(BF16)
            for parity in range(2):
                out_ref[4 * h + 2 * two + parity] = both[parity * HALF : (parity + 1) * HALF, :]


def reduce_and_solve(table, window, blocks, forward, skel, parent):
    return pl.pallas_call(
        reduce_kernel,
        out_shape=(shape(8, 64, 128), shape(*window.shape)),
        in_specs=[SMEM] + [VMEM] * 9,
        out_specs=[VMEM] * 2,
        input_output_aliases={1: 1},
        name="reduce_and_solve",
        cost_estimate=cost(2 * 16 * 64 * 1536 * 128, 6000000),
        compiler_params=limit(6),
    )(table, window, *blocks, *forward, *skel, *parent)[0]


def own_kernel(own_ref, *refs):
    tail_refs, base_refs, out_ref = refs[:2], refs[2:4], refs[4]
    low = low_lanes()
    for h in range(2):
        for pair in range(4):
            own = own_ref[4 * h + pair].astype(F32)
            for t in range(2):
                j = 2 * pair + t
                tail = jnp.where(low, 0.0, turned(own) if t == 0 else own).astype(BF16)
                out_ref[8 * h + j] = base_refs[h][j] + lax.dot_general(
                    tail, tail_refs[h][j], NT, preferred_element_type=F32
                )


def add_own(own, tails, base):
    return pl.pallas_call(
        own_kernel,
        out_shape=shape(16, 64, 256, dtype=F32),
        in_specs=[VMEM] * 5,
        out_specs=VMEM,
        name="add_own",
        cost_estimate=cost(2 * 16 * 64 * 128 * 256, 4000000),
        compiler_params=limit(4),
    )(own, *tails, *base)


def finish_kernel(table_ref, *refs):
    blocks, wide_refs, base_ref, out_ref, window = refs[:5], refs[5:7], refs[7], refs[8], refs[9]
    for n, block in enumerate(blocks):
        place_block(window, block, 8 * n)
    window[2 * ROWS] = jnp.zeros(window.shape[1:], BF16)
    core = lax.axis_index("rhs")
    low = low_lanes()
    for h in range(2):
        for j in range(8):
            cluster = (core ^ h) * 8 + j
            parts = []
            for k in range(0, 8, 2):
                left, right = window[table_ref[k, cluster]], window[table_ref[k + 1, cluster]]
                parts.append(jnp.where(low, left, right))
            carried = lax.dot_general(
                jnp.concatenate(parts, axis=1), wide_refs[h][j], NT, preferred_element_type=F32
            )
            out_ref[cluster] = (base_ref[8 * h + j] - carried).astype(BF16)


def finish(table, blocks, wide, base):
    return pl.pallas_call(
        finish_kernel,
        out_shape=shape(16, 64, 256),
        in_specs=[SMEM] + [VMEM] * 8,
        out_specs=VMEM,
        scratch_shapes=[pltpu.VMEM((2 * ROWS + 1, 64, 128), BF16)],
        name="finish",
        cost_estimate=cost(2 * 16 * 64 * 512 * 256, 6000000),
        compiler_params=limit(6),
    )(table, *blocks, *wide, base)


def on_device(
    rhs_block,
    basis,
    red_inverse,
    forward_coupling,
    backward_coupling,
    parent_inverse,
    near_index,
    near_count,
):
    inner, outer, near, far = leaf_pairs(lax.axis_size("leaf"))
    basis_b = swap(basis)
    inverse_b = swap(red_inverse)
    elim_a, skel_a, rest, basis_a, inverse_a = project_own(rhs_block, basis, red_inverse)
    inner_a = along(elim_a, inner)
    outer_a = along(elim_a, outer)
    elim_b, skel_b = project_other(rest, basis_b, inverse_b)
    inner_b = along(elim_b, inner)
    outer_b = along(elim_b, outer)
    parent_b = swap(parent_inverse)
    forward_b = swap(forward_coupling)
    backward_b = swap(backward_coupling)
    far_outer_a = along(inner_a, outer)
    far_inner_a = along(outer_a, inner)
    far_outer_b = along(inner_b, outer)
    far_inner_b = along(outer_b, inner)
    forward_table, backward_table = tables(near_index, near_count)
    window_blocks = (elim_a, elim_b, inner_a, inner_b, outer_a, outer_b)
    window = gather((0, 4, 8, 12, 16, 20), window_blocks)
    window = gather((24, 32), (far_inner_a, far_outer_a), window)
    wide_a, base_a, tail_a = fold(elim_a, inverse_a, basis_a, backward_coupling)
    wide_b, base_b, tail_b = fold(elim_b, inverse_b, basis_b, backward_b)
    factors = (forward_coupling, forward_b), (skel_a, skel_b), (parent_inverse, parent_b)
    skeleton = reduce_and_solve(forward_table, window, (far_inner_b, far_outer_b), *factors)
    near_s = along(skeleton, near)
    inner_s = along(skeleton, inner)
    far_s = along(skeleton, far)
    outer_s = along(skeleton, outer)
    base = add_own(skeleton, (tail_a, tail_b), (base_a, base_b))
    return finish(backward_table, (skeleton, inner_s, outer_s, near_s, far_s), (wide_a, wide_b), base)


def solution(mesh):
    whole = P(("leaf", "rhs"), None, None)
    in_specs = (P("leaf", "rhs", None), whole, whole, whole, whole, whole, P("leaf", None), P("leaf"))
    return jax.shard_map(
        on_device, mesh=mesh, in_specs=in_specs, out_specs=P("leaf", "rhs", None), check_vma=False
    )
```

```python
import functools

import jax
import jax.numpy as jnp
from jax import lax
from jax.experimental import pallas as pl
from jax.experimental.pallas import tpu as pltpu
from jax.sharding import PartitionSpec as P


HALF = 64
ROWS = 40
F32 = jnp.float32
BF16 = jnp.bfloat16
NT = (((1,), (1,)), ((), ()))
TN = (((0,), (0,)), ((), ()))
SMEM = pl.BlockSpec(memory_space=pltpu.SMEM)
VMEM = pl.BlockSpec(memory_space=pltpu.VMEM)
HBM = pl.BlockSpec(memory_space=pltpu.HBM)


def shape(*dims, dtype=BF16):
    return jax.ShapeDtypeStruct(dims, dtype)


def cost(flops, moved):
    return pl.CostEstimate(flops=flops, bytes_accessed=moved, transcendentals=0)


def limit(mebibytes):
    return pltpu.CompilerParams(vmem_limit_bytes=mebibytes << 20)


def in_hbm(*values):
    return [pltpu.with_memory_space_constraint(value, pltpu.HBM) for value in values]


def both_ways(pairs):
    return [(a, b) for a, b in pairs] + [(b, a) for a, b in pairs]


def leaf_pairs(count):
    inner = both_ways([(i, i + 1) for i in range(0, count - 1, 2)])
    outer = both_ways([(i, i + 1) for i in range(1, count - 1, 2)])
    near = both_ways([(i, i + 2) for i in range(count - 2) if i % 4 in (0, 1)])
    far = both_ways([(i, i + 2) for i in range(count - 2) if i % 4 in (2, 3)])
    return inner, outer, near, far


def swap(value):
    return lax.ppermute(value, "rhs", [(0, 1), (1, 0)])


def along(value, pairs):
    return lax.ppermute(value, "leaf", pairs)


def low_lanes():
    return lax.broadcasted_iota(jnp.int32, (1, 2 * HALF), 1) < HALF


def turned(value):
    return pltpu.roll(value, HALF, 1)


def tables_kernel(near_ref, count_ref, forward_ref, backward_ref):
    leaf, core = lax.axis_index("leaf"), lax.axis_index("rhs")
    sign = 1 - 2 * (leaf & 1)
    flip = jnp.where((leaf & 3 == 1) | (leaf & 3 == 2), 7, 0)
    target = near_ref[...]
    slot = lax.broadcasted_iota(jnp.int32, target.shape, 0)
    cluster = lax.broadcasted_iota(jnp.int32, target.shape, 1)
    used = slot < count_ref[...]
    away = (lax.shift_right_logical(target, 4) - leaf) * sign
    block = jnp.where(away > 0, 2 * away - 1, -2 * away)
    other = jnp.where(block >= 3, block ^ flip, block)
    inside = target & 15
    place = lax.shift_right_logical(inside ^ (core << 3), 1)
    side = inside & 1
    forward = block * 8 + place + (side ^ (lax.shift_right_logical(cluster, 1) & 1)) * ROWS
    backward = other * 8 + place + (side ^ (slot & 1)) * ROWS
    forward_ref[...] = jnp.where(used, forward, 2 * ROWS)
    backward_ref[...] = jnp.where(used, backward, 2 * ROWS)


def tables(near_index, near_count):
    slots = near_index.T
    return pl.pallas_call(
        tables_kernel,
        out_shape=[shape(*slots.shape, dtype=jnp.int32)] * 2,
        in_specs=[VMEM] * 2,
        out_specs=[VMEM] * 2,
        name="tables",
        cost_estimate=cost(10000, 10000),
        compiler_params=limit(1),
    )(slots, near_count.reshape(1, -1))


def project_pair(pair, base, rhs_ref, basis_ref, inverse_ref, elim_ref, skel_ref):
    redundant = inverse_ref.shape[1]
    zeros = jnp.zeros((HALF, redundant), BF16)
    elim = None
    tails = []
    for t in range(2):
        j = 2 * pair + t
        projected = jnp.dot(rhs_ref[base + j], basis_ref[j], preferred_element_type=F32)
        head = projected[:, :redundant].astype(BF16)
        tails.append(projected[:, 128:])
        stack = [head, zeros] if t == 0 else [zeros, head]
        part = lax.dot_general(
            inverse_ref[j], jnp.concatenate(stack, axis=0), NT, preferred_element_type=F32
        )
        elim = part if elim is None else elim + part
    elim_ref[pair] = elim.astype(BF16)
    skel_ref[pair] = jnp.concatenate(tails, axis=0).T[HALF:, :]


def project_own_kernel(
    rhs_hbm, basis_hbm, inverse_hbm, elim_ref, skel_ref, rest_ref, basis, inverse, rhs, sems, rest_sem
):
    core = lax.axis_index("rhs")
    base = core * 8
    copies = []
    for pair in range(4):
        here = pl.ds(2 * pair, 2)
        group = [
            pltpu.make_async_copy(rhs_hbm.at[pl.ds(base + 2 * pair, 2)], rhs.at[here], sems.at[pair, 0]),
            pltpu.make_async_copy(basis_hbm.at[here], basis.at[here], sems.at[pair, 1]),
            pltpu.make_async_copy(inverse_hbm.at[here], inverse.at[here], sems.at[pair, 2]),
        ]
        for copy in group:
            copy.start()
        copies.append(group)
    rest = pltpu.make_async_copy(rhs_hbm.at[pl.ds(8 - base, 8)], rest_ref, rest_sem)
    rest.start()
    for group in copies:
        for copy in group:
            copy.wait()
    for pair in range(4):
        project_pair(pair, 0, rhs, basis, inverse, elim_ref, skel_ref)
    rest.wait()


def project_own(rhs_block, basis, inverse):
    return pl.pallas_call(
        project_own_kernel,
        out_shape=[
            shape(4, 192, 128),
            shape(4, 64, 128, dtype=F32),
            shape(8, *rhs_block.shape[1:]),
            shape(*basis.shape),
            shape(*inverse.shape),
        ],
        in_specs=[HBM] * 3,
        out_specs=[VMEM] * 5,
        scratch_shapes=[
            pltpu.VMEM((8,) + rhs_block.shape[1:], BF16),
            pltpu.SemaphoreType.DMA((4, 3)),
            pltpu.SemaphoreType.DMA(()),
        ],
        name="project_own",
        cost_estimate=cost(2 * 8 * 64 * (65536 + 36864), 2500000),
        compiler_params=limit(8),
    )(*in_hbm(rhs_block, basis, inverse))


def project_other_kernel(rhs_ref, basis_ref, inverse_ref, elim_ref, skel_ref):
    for pair in range(4):
        project_pair(pair, 0, rhs_ref, basis_ref, inverse_ref, elim_ref, skel_ref)


def project_other(rhs_block, basis, inverse):
    return pl.pallas_call(
        project_other_kernel,
        out_shape=[shape(4, 192, 128), shape(4, 64, 128, dtype=F32)],
        in_specs=[VMEM] * 3,
        out_specs=[VMEM] * 2,
        name="project_other",
        cost_estimate=cost(2 * 8 * 64 * (65536 + 36864), 2500000),
        compiler_params=limit(6),
    )(rhs_block, basis, inverse)


def place_block(window, block, first):
    for pair in range(block.shape[0]):
        value = block[pair]
        window[first + pair] = value
        window[first + pair + ROWS] = turned(value)


def gather_kernel(firsts, fresh, *refs):
    window = refs[-1]
    blocks = refs[:-1] if fresh else refs[1:-1]
    for first, block in zip(firsts, blocks):
        place_block(window, block, first)
    if fresh:
        window[2 * ROWS] = jnp.zeros(window.shape[1:], BF16)


def gather(firsts, blocks, window=None):
    fresh = window is None
    operands = blocks if fresh else (window,) + blocks
    return pl.pallas_call(
        functools.partial(gather_kernel, firsts, fresh),
        out_shape=shape(2 * ROWS + 1, *blocks[0].shape[1:]),
        in_specs=[VMEM] * len(operands),
        out_specs=VMEM,
        input_output_aliases={} if fresh else {0: 0},
        name="gather",
        cost_estimate=cost(1000, 4000000),
        compiler_params=limit(6),
    )(*operands)


def fold_kernel(elim_ref, inverse_ref, basis_ref, backward_ref, wide_ref, base_ref, tail_ref):
    redundant = inverse_ref.shape[1]
    for pair in range(4):
        elim = elim_ref[pair].astype(F32).T.astype(BF16)
        for t in range(2):
            j = 2 * pair + t
            both = lax.dot_general(
                inverse_ref[j], basis_ref[j][:, :redundant], NT, preferred_element_type=F32
            ).astype(BF16)
            wide_ref[j] = lax.dot_general(
                backward_ref[j], both, TN, preferred_element_type=F32
            ).astype(BF16)
            base_ref[j] = jnp.dot(
                elim[t * HALF : (t + 1) * HALF, :], both, preferred_element_type=F32
            )
            tail_ref[j] = basis_ref[j][:, 128:]


def fold(elim, inverse, basis, backward):
    return pl.pallas_call(
        fold_kernel,
        out_shape=(shape(8, 512, 256), shape(8, 64, 256, dtype=F32), shape(8, 256, 128)),
        in_specs=[VMEM] * 4,
        out_specs=[VMEM] * 3,
        name="fold",
        cost_estimate=cost(2 * 8 * 256 * 192 * 768, 8000000),
        compiler_params=limit(6),
    )(elim, inverse, basis, backward)


def reduce_kernel(table_ref, window_in, *refs):
    last_ref, *refs = refs
    f_refs, skel_refs, parent_refs = refs[:2], refs[2:4], refs[4:6]
    out_ref, window = refs[6:]
    core = lax.axis_index("rhs")
    place_block(window, last_ref, 36)
    low = low_lanes()
    for h in range(2):
        for two in range(2):
            solved = []
            for parity in range(2):
                pair = 2 * two + parity
                skel = skel_refs[h][pair]
                reduced = []
                for t in range(2):
                    j = 2 * pair + t
                    parts = [window[table_ref[k, (core ^ h) * 8 + j]] for k in range(8)]
                    total = jnp.dot(
                        f_refs[h][j], jnp.concatenate(parts, axis=0), preferred_element_type=F32
                    )
                    reduced.append(((skel if t == parity else turned(skel)) - total).astype(BF16))
                solved.append(
                    jnp.dot(
                        parent_refs[h][pair], jnp.concatenate(reduced, axis=0), preferred_element_type=F32
                    )
                )
            both = jnp.where(low, solved[0], solved[1]).T.astype(BF16)
            for parity in range(2):
                out_ref[4 * h + 2 * two + parity] = both[parity * HALF : (parity + 1) * HALF, :]


def reduce_and_solve(table, window, last, forward, skel, parent):
    return pl.pallas_call(
        reduce_kernel,
        out_shape=(shape(8, 64, 128), shape(*window.shape)),
        in_specs=[SMEM] + [VMEM] * 8,
        out_specs=[VMEM] * 2,
        input_output_aliases={1: 1},
        name="reduce_and_solve",
        cost_estimate=cost(2 * 16 * 64 * 1536 * 128, 6000000),
        compiler_params=limit(6),
    )(table, window, last, *forward, *skel, *parent)[0]


def own_kernel(own_ref, *refs):
    tail_refs, base_refs, out_ref = refs[:2], refs[2:4], refs[4]
    low = low_lanes()
    for h in range(2):
        for pair in range(4):
            own = own_ref[4 * h + pair].astype(F32)
            for t in range(2):
                j = 2 * pair + t
                tail = jnp.where(low, 0.0, turned(own) if t == 0 else own).astype(BF16)
                out_ref[8 * h + j] = base_refs[h][j] + lax.dot_general(
                    tail, tail_refs[h][j], NT, preferred_element_type=F32
                )


def add_own(own, tails, base):
    return pl.pallas_call(
        own_kernel,
        out_shape=shape(16, 64, 256, dtype=F32),
        in_specs=[VMEM] * 5,
        out_specs=VMEM,
        name="add_own",
        cost_estimate=cost(2 * 16 * 64 * 128 * 256, 4000000),
        compiler_params=limit(4),
    )(own, *tails, *base)


def finish_kernel(row, table_ref, window_in, last_ref, *refs):
    wide_refs, base_ref = refs[:2], refs[2]
    out_hbm, window, out_ref, sems = refs[3:]
    place_block(window, last_ref, row)
    core = lax.axis_index("rhs")
    low = low_lanes()
    copies = []
    for h in range(2):
        for j in range(8):
            cluster = (core ^ h) * 8 + j
            parts = []
            for k in range(0, 8, 2):
                left, right = window[table_ref[k, cluster]], window[table_ref[k + 1, cluster]]
                parts.append(jnp.where(low, left, right))
            carried = jnp.dot(
                jnp.concatenate(parts, axis=1), wide_refs[h][j], preferred_element_type=F32
            )
            out_ref[8 * h + j] = (base_ref[8 * h + j] - carried).astype(BF16)
        here = pl.ds((core ^ h) * 8, 8)
        copies.append(pltpu.make_async_copy(out_ref.at[pl.ds(8 * h, 8)], out_hbm.at[here], sems.at[h]))
        copies[h].start()
    for copy in copies:
        copy.wait()


def finish(row, table, window, last, wide, base):
    return pl.pallas_call(
        functools.partial(finish_kernel, row),
        out_shape=(shape(*base.shape), shape(*window.shape)),
        in_specs=[SMEM] + [VMEM] * 5,
        out_specs=(HBM, VMEM),
        scratch_shapes=[pltpu.VMEM(base.shape, BF16), pltpu.SemaphoreType.DMA((2,))],
        input_output_aliases={1: 1},
        name="finish",
        cost_estimate=cost(2 * 16 * 64 * 512 * 256, 6000000),
        compiler_params=pltpu.CompilerParams(vmem_limit_bytes=6 << 20),
    )(table, window, last, *wide, base)[0]


def on_device(
    rhs_block,
    basis,
    red_inverse,
    forward_coupling,
    backward_coupling,
    parent_inverse,
    near_index,
    near_count,
):
    inner, outer, near, far = leaf_pairs(lax.axis_size("leaf"))
    basis_b = swap(basis)
    inverse_b = swap(red_inverse)
    elim_a, skel_a, rest, basis_a, inverse_a = project_own(rhs_block, basis, red_inverse)
    inner_a = along(elim_a, inner)
    outer_a = along(elim_a, outer)
    elim_b, skel_b = project_other(rest, basis_b, inverse_b)
    inner_b = along(elim_b, inner)
    outer_b = along(elim_b, outer)
    parent_b = swap(parent_inverse)
    forward_b = swap(forward_coupling)
    backward_b = swap(backward_coupling)
    far_outer_a = along(inner_a, outer)
    far_inner_a = along(outer_a, inner)
    far_outer_b = along(inner_b, outer)
    far_inner_b = along(outer_b, inner)
    forward_table, backward_table = tables(near_index, near_count)
    window_blocks = (elim_a, elim_b, inner_a, inner_b, outer_a, outer_b)
    window = gather((0, 4, 8, 12, 16, 20), window_blocks)
    window = gather((24, 32), (far_inner_a, far_outer_a), window)
    window = gather((28,), (far_inner_b,), window)
    wide_a, base_a, tail_a = fold(elim_a, inverse_a, basis_a, backward_coupling)
    wide_b, base_b, tail_b = fold(elim_b, inverse_b, basis_b, backward_b)
    factors = (forward_coupling, forward_b), (skel_a, skel_b), (parent_inverse, parent_b)
    skeleton = reduce_and_solve(forward_table, window, far_outer_b, *factors)
    near_s = along(skeleton, near)
    inner_s = along(skeleton, inner)
    far_s = along(skeleton, far)
    outer_s = along(skeleton, outer)
    base = add_own(skeleton, (tail_a, tail_b), (base_a, base_b))
    window = gather((0, 8, 16, 32), (skeleton, inner_s, outer_s, far_s))
    return finish(24, backward_table, window, near_s, (wide_a, wide_b), base)


def solution(mesh):
    whole = P(("leaf", "rhs"), None, None)
    in_specs = (P("leaf", "rhs", None), whole, whole, whole, whole, whole, P("leaf", None), P("leaf"))
    return jax.shard_map(
        on_device, mesh=mesh, in_specs=in_specs, out_specs=P("leaf", "rhs", None), check_vma=False
    )
```
